32 devices in a mesh: groups: 2 (over x), slab: 4 (over y, core), view: 4 (over z).
Axes of the slice: x: 2, y: 2, z: 4, core: 2. Of those that a mesh axis runs over, the one named last changes fastest.
Arguments:
- estimate: float32 [128, 64, 256], P(('groups', 'slab')), parts along dimension 0, may hold values from 0.3 to 3
- measured: float32 [8, 128, 64, 256], P('view', ('groups', 'slab')), parts along dimension 1, may hold values from 0.2 to 5
- psf_z: float32 [8, 4, 15], P('view'), may hold values from 0.01 to 1
- psf_y: float32 [8, 4, 15], P('view'), may hold values from 0.01 to 1
- psf_x: float32 [8, 4, 15], P('view'), may hold values from 0.01 to 1
- weight_table: float32 [4], replicated, may hold values from 0.1 to 1
- weight_index: int32 [8], replicated, may hold values from 0 to 3
Outputs:
- new_estimate: float32 [128, 64, 256], P(('groups', 'slab')), parts along dimension 0
The draws below stay inside these ranges and needn't reach their ends.
There are 2 independent parts, one for each index of `groups`. The reference program is written for one: setup_inputs(seed, part) draws one part's arguments, and reference() takes and returns one part's arrays. A program takes and returns all parts, laid end to end along the dimension named above; an argument that names none is the same for every part. Nothing has to cross between parts.
All inputs are finite; a program needn't handle non-finite values.
Results may differ from the reference program's by a relative error of at most 0.000068.
Values sent between devices are 32-bit elements; how exact they have to be, the bound alone decides.
No kernel may reach another device: no remote copies, remote signals or barrier semaphores. Data moves between devices by JAX's collectives and lax.ppermute only.
A program may use at most 64 MiB of HBM per device.

```python
import math
import jax
import jax.numpy as jnp
from jax import lax

Y = 64
X = 256
TAPS = 15
RANK = 4
LEVELS = 4
VIEWS = 8
Z = 64


def with_ends(result, own_key, smallest, high):
    dims = result.shape
    place = [jax.random.randint(jax.random.fold_in(own_key, axis), (), 0, dims[axis]) for axis in range(len(dims))]
    result = result.at[tuple(place)].set(smallest)
    longest = dims.index(max(dims))
    place[longest] = (place[longest] + 1) % dims[longest]
    return result.at[tuple(place)].set(high)


def level_of(own_key, dims, split, least, largest):
    loudness = 1.0
    for position, shards_of in split:
        heights = jax.random.uniform(jax.random.fold_in(jax.random.fold_in(own_key, 6), position), (shards_of,), jnp.float32, least / len(split), largest / len(split))
        loudness = loudness * jnp.repeat(jnp.exp(heights), dims[position] // shards_of).reshape((-1,) + (1,) * (len(dims) - 1 - position))
    return loudness


def setup_inputs(seed: int = 0, part: int = 0) -> dict:
    seeds = jax.random.split(jax.random.key(seed), 8)
    part_splits = jax.random.split(jax.random.fold_in(seeds[7], part), 8)
    estimate = jnp.clip(jnp.exp(math.log(3.0) - 2.3025851 * jax.random.uniform(part_splits[0], (Z, Y, X), jnp.float32) ** level_of(part_splits[0], (Z, Y, X), ((0, 4),), -0.2, 0.2)), 0.3, 3.0)
    measured = jnp.clip(jnp.exp(math.log(5.0) - 3.218876 * jax.random.uniform(part_splits[1], (VIEWS, Z, Y, X), jnp.float32) ** level_of(part_splits[1], (VIEWS, Z, Y, X), ((0, 4), (1, 4)), -0.2, 0.2)), 0.2, 5.0)
    psf_z = jnp.clip(jnp.exp(math.log(1.0) - 4.6051702 * jax.random.uniform(seeds[2], (VIEWS, RANK, TAPS), jnp.float32) ** level_of(seeds[2], (VIEWS, RANK, TAPS), ((0, 4),), -0.2, 0.2)), 0.01, 1.0)
    psf_y = jnp.clip(jnp.exp(math.log(1.0) - 4.6051702 * jax.random.uniform(seeds[3], (VIEWS, RANK, TAPS), jnp.float32) ** level_of(seeds[3], (VIEWS, RANK, TAPS), ((0, 4),), -0.2, 0.2)), 0.01, 1.0)
    psf_x = jnp.clip(jnp.exp(math.log(1.0) - 4.6051702 * jax.random.uniform(seeds[4], (VIEWS, RANK, TAPS), jnp.float32) ** level_of(seeds[4], (VIEWS, RANK, TAPS), ((0, 4),), -0.2, 0.2)), 0.01, 1.0)
    weight_table = jnp.clip(jnp.exp(jax.random.uniform(seeds[5], (LEVELS,), jnp.float32, math.log(0.1), math.log(1.0))), 0.1, 1.0)
    weight_index = with_ends(jax.random.randint(seeds[6], (VIEWS,), 0, LEVELS), jax.random.fold_in(seeds[6], 1), 0, LEVELS - 1).astype(jnp.int32)
    return {"estimate": estimate, "measured": measured, "psf_z": psf_z, "psf_y": psf_y, "psf_x": psf_x, "weight_table": weight_table, "weight_index": weight_index}


def along_axis(volume, kernel, which_axis, adjoint):
    radius = (kernel.shape[0] - 1) // 2
    length = volume.shape[which_axis]
    widths = [(0, 0)] * volume.ndim
    widths[which_axis] = (radius, radius)
    padded = jnp.pad(volume, widths)
    summed = jnp.zeros_like(volume)
    for tap_pos in range(kernel.shape[0]):
        anchor = 2 * radius - tap_pos if adjoint else tap_pos
        summed = summed + kernel[tap_pos] * lax.slice_in_dim(padded, anchor, anchor + length, axis=which_axis)
    return summed


def reference(estimate, measured, psf_z, psf_y, psf_x, weight_table, weight_index):
    levels = jnp.arange(weight_table.shape[0], dtype=jnp.int32)
    weights = jnp.sum(jnp.where(weight_index[:, None] == levels[None, :], weight_table[None, :], jnp.zeros_like(weight_table)[None, :]), axis=1)
    accum = jnp.zeros_like(estimate)
    for member in range(VIEWS):
        blurred = jnp.zeros_like(estimate)
        for term in range(RANK):
            inner = along_axis(estimate, psf_x[member, term], 2, False)
            inner = along_axis(inner, psf_y[member, term], 1, False)
            blurred = blurred + along_axis(inner, psf_z[member, term], 0, False)
        ratio = measured[member] / blurred
        back = jnp.zeros_like(estimate)
        normal = jnp.zeros_like(estimate)
        for term in range(RANK):
            inner = along_axis(ratio, psf_z[member, term], 0, True)
            inner = along_axis(inner, psf_y[member, term], 1, True)
            back = back + along_axis(inner, psf_x[member, term], 2, True)
            col_z = along_axis(jnp.ones((estimate.shape[0],), estimate.dtype), psf_z[member, term], 0, True)
            col_y = along_axis(jnp.ones((estimate.shape[1],), estimate.dtype), psf_y[member, term], 0, True)
            col_x = along_axis(jnp.ones((estimate.shape[2],), estimate.dtype), psf_x[member, term], 0, True)
            normal = normal + col_z[:, None, None] * col_y[None, :, None] * col_x[None, None, :]
        accum = accum + weights[member] * (back / normal)
    return estimate * (accum / jnp.sum(weights))
```

```python
import functools

import jax
import jax.numpy as jnp
from jax import lax
from jax.experimental import pallas as pl
from jax.experimental.pallas import tpu as pltpu
from jax.sharding import PartitionSpec as P

f32 = jnp.float32
bf16 = jnp.bfloat16
SUB = 8
VMEM_LIMIT = 24 * 2**20


def split(values):
    high = values.astype(bf16)
    return high, (values - high.astype(f32)).astype(bf16)


def dot(a, b):
    return jnp.dot(a, b, preferred_element_type=f32)


def skew(row, rows, shift):
    width = row.shape[1]
    full = jnp.broadcast_to(row, (rows, width))
    return pltpu.roll(full, shift % width, 1, stride=1, stride_axis=0)


def tap_row(ref, place, width, start, step, flip):
    taps = ref.shape[-1]
    lane = lax.broadcasted_iota(jnp.int32, (1, width), 1)
    row = jnp.zeros((1, width), f32)
    for k in range(taps):
        value = ref[place + (taps - 1 - k if flip else k,)]
        row = jnp.where(lane == start + k * step, value, row)
    return row


def prep_kernel(chunk, psf_z, psf_y, psf_x, table, index, est, xh, xl, ym, zm, scale):
    members, rank, taps = psf_x.shape
    planes, height, width = est.shape
    radius = (taps - 1) // 2
    packed = rank * height
    first = lax.axis_index("slab") * planes
    total = lax.axis_size("slab") * planes
    view = lax.axis_index("view")

    def weight_of(v):
        code = index[v]
        weight = jnp.float32(0)
        for level in range(table.shape[0]):
            weight = weight + jnp.where(code == level, table[level], jnp.float32(0))
        return weight

    grand = jnp.float32(0)
    for v in range(index.shape[0]):
        grand = grand + weight_of(v)
    q = lax.broadcasted_iota(jnp.int32, (width, width), 0)
    p = lax.broadcasted_iota(jnp.int32, (width, width), 1)
    band = jnp.abs(p - q) <= radius
    yp = lax.broadcasted_iota(jnp.int32, (height, packed), 0)
    lane = lax.broadcasted_iota(jnp.int32, (height, packed), 1)
    yband = jnp.abs(lax.rem(lane, height) - yp) <= radius
    depth = first + lax.broadcasted_iota(jnp.int32, (planes, width), 0)
    for m in range(members):
        for way in range(2):
            slot = 2 * m + way
            flip = way == 0
            col_x = []
            for r in range(rank):
                mat = jnp.where(band, skew(tap_row(psf_x, (m, r), width, 0, 1, flip), width, -radius), 0.0)
                high, low = split(mat)
                xh[slot, r] = high
                xl[slot, r] = low
                if way:
                    col_x.append(jnp.sum(mat, axis=0, keepdims=True))
            row = jnp.zeros((1, packed), f32)
            for r in range(rank):
                row = row + tap_row(psf_y, (m, r), packed, r * height, 1, not flip)
            ymat = jnp.where(yband, skew(row, height, -radius), 0.0)
            high, low = split(ymat)
            ym[slot] = jnp.concatenate([high, low], axis=0)
            zmat = jnp.concatenate(
                [skew(tap_row(psf_z, (m, r), zm.shape[2], 0, SUB, not flip), chunk * SUB, 0) for r in range(rank)],
                axis=0,
            )
            high, low = split(zmat)
            zm[slot] = jnp.concatenate([high, low], axis=0)
        shares = []
        for r in range(rank):
            own = (lane >= r * height) & (lane < (r + 1) * height)
            col_y = jnp.sum(jnp.where(own, ymat, 0.0), axis=1, keepdims=True)
            col_z = jnp.zeros((planes, width), f32)
            for k in range(taps):
                source = depth + (radius - k)
                inside = (source >= 0) & (source < total)
                col_z = col_z + jnp.where(inside, psf_z[m, r, k], 0.0)
            shares.append((col_z, col_y * col_x[r]))
        weight = weight_of(view * members + m)
        for z in range(planes):
            normal = jnp.zeros((height, width), f32)
            for col_z, outer in shares:
                normal = normal + col_z[z : z + 1] * outer
            scale[m, z] = est[z] * (weight / (grand * normal))


def load_split(pieces, first, last, high, low):
    starts = [0]
    for piece in pieces:
        starts.append(starts[-1] + piece.shape[0])
    for block in range(high.shape[0]):
        parts = []
        for piece, start in zip(pieces, starts):
            a, b = max(first - start, 0), min(last - start, piece.shape[0])
            if a < b:
                parts.append(piece[a:b, block * SUB : (block + 1) * SUB, :])
        rows = jnp.concatenate(parts, axis=0)
        rows = rows.reshape((last - first) * SUB, rows.shape[2])
        h, l = split(rows)
        high[block, 0 : rows.shape[0]] = h
        low[block, 0 : rows.shape[0]] = l


def apply_chunk(c, chunk, reach, high, low, mats, scratch):
    xh, xl, ym, zm = mats
    dh, dl, f = scratch
    rank, width = xh.shape[0], xh.shape[1]
    blocks = high.shape[0]
    height = blocks * SUB
    depth = (chunk + reach) * SUB
    rows = chunk * SUB
    stacked = rank * rows
    zmat = zm[:, 0:depth]
    window = pl.ds(c * rows if isinstance(c, int) else pl.multiple_of(c * rows, rows), depth)
    for block in range(blocks):
        hw = high[block, window, :]
        lw = low[block, window, :]
        both = dot(zmat, hw)
        d = both[:stacked] + both[stacked:] + dot(zmat[:stacked], lw)
        for r in range(rank):
            h, l = split(d[r * rows : (r + 1) * rows])
            dh[r, block * rows : (block + 1) * rows] = h
            dl[r, block * rows : (block + 1) * rows] = l
    for r in range(rank):
        f[r] = dot(dh[r], xh[r]) + dot(dl[r], xh[r]) + dot(dh[r], xl[r])
    results = []
    for z in range(chunk):
        plane = [f[r].reshape(blocks, chunk, SUB, width)[:, z].reshape(height, width) for r in range(rank)]
        h, l = split(jnp.concatenate(plane, axis=0))
        both = dot(ym[...], h)
        results.append(both[:height] + both[height:] + dot(ym[0:height], l))
    return results


def forward_kernel(chunk, reach, before, est, after, measured, *rest):
    mats, (ratio, head, tail, high, low, *scratch) = rest[:4], rest[4:]
    c = pl.program_id(0)
    planes = ratio.shape[0]

    @pl.when(c == 0)
    def _():
        load_split((before, est, after), 0, planes + reach, high, low)

    blurred = apply_chunk(c, chunk, reach, high, low, mats, scratch)
    for z in range(chunk):
        ratio[c * chunk + z] = measured[z] / blurred[z]

    @pl.when(c == pl.num_programs(0) - 1)
    def _():
        head[...] = ratio[0 : head.shape[0]]
        tail[...] = ratio[planes - tail.shape[0] : planes]


def backward_kernel(chunk, reach, first, count, views, has_sum, has_after, *refs):
    refs = list(refs)
    take = lambda n: [refs.pop(0) for _ in range(n)]
    per_view = [(take(3), take(1)[0], take(4)) for _ in range(views)]
    running = take(1)[0] if has_sum else None
    if has_after:
        take(1)
    (out,) = take(1)
    high, low, *scratch = refs
    for i, (pieces, scale, mats) in enumerate(per_view):
        load_split(pieces, first * chunk, (first + count) * chunk + reach, high, low)
        for c in range(count):
            back = apply_chunk(c, chunk, reach, high, low, mats, scratch)
            for z in range(chunk):
                term = back[z] * scale[c * chunk + z]
                if i:
                    term = term + out[c * chunk + z]
                elif has_sum:
                    term = term + running[z]
                out[c * chunk + z] = term


def whole(shape):
    return pl.BlockSpec(shape, lambda *_: (0,) * len(shape))


def slot_of(array, slot):
    return pl.BlockSpec((None,) + array.shape[1:], lambda *_: (slot,) + (0,) * (array.ndim - 1))


def per_device(estimate, measured, psf_z, psf_y, psf_x, weight_table, weight_index):
    members, planes, height, width = measured.shape
    rank, taps = psf_x.shape[1:]
    reach = taps - 1
    radius = reach // 2
    chunk = next(c for c in (4, 2, 1) if planes % c == 0)
    chunks = planes // chunk
    struct = jax.ShapeDtypeStruct
    plane = (height, width)
    params = pltpu.CompilerParams(vmem_limit_bytes=VMEM_LIMIT)
    smem = pl.BlockSpec(memory_space=pltpu.SMEM)

    slabs = lax.axis_size("slab")
    up = [(i, i + 1) for i in range(slabs - 1)]
    down = [(i + 1, i) for i in range(slabs - 1)]

    def cost(fraction):
        flops = 2 * 6912 * 65536 * chunks * fraction
        return pl.CostEstimate(flops=int(flops), bytes_accessed=int(4e6), transcendentals=0)

    before = lax.ppermute(estimate[planes - radius :], "slab", up)
    after = lax.ppermute(estimate[:radius], "slab", down)
    depth_lanes = -(-(chunk + reach) * SUB // 128) * 128
    slots = 2 * members
    mats_and_scale = pl.pallas_call(
        functools.partial(prep_kernel, chunk),
        out_shape=[
            struct((slots, rank, width, width), bf16),
            struct((slots, rank, width, width), bf16),
            struct((slots, 2 * height, rank * height), bf16),
            struct((slots, 2 * rank * chunk * SUB, depth_lanes), bf16),
            struct((members, planes) + plane, f32),
        ],
        in_specs=[smem] * 5 + [pl.BlockSpec(memory_space=pltpu.VMEM)],
        compiler_params=params,
        cost_estimate=cost(0.7),
        name="prep",
    )(psf_z, psf_y, psf_x, weight_table, weight_index, estimate)
    mats, scale = mats_and_scale[:4], mats_and_scale[4]

    def work(window):
        return [
            pltpu.VMEM((height // SUB, window * SUB, width), bf16),
            pltpu.VMEM((height // SUB, window * SUB, width), bf16),
            pltpu.VMEM((rank, height * chunk, width), bf16),
            pltpu.VMEM((rank, height * chunk, width), bf16),
            pltpu.VMEM((rank, height * chunk, width), f32),
        ]

    extended = []
    for m in range(members):
        ratio, head, tail = pl.pallas_call(
            functools.partial(forward_kernel, chunk, reach),
            grid=(chunks,),
            out_shape=[struct((planes,) + plane, f32), struct((radius,) + plane, f32), struct((radius,) + plane, f32)],
            in_specs=[
                whole(before.shape),
                whole(estimate.shape),
                whole(after.shape),
                pl.BlockSpec((None, chunk) + plane, lambda c, m=m: (m, c, 0, 0)),
            ]
            + [slot_of(a, 2 * m) for a in mats],
            out_specs=[whole((planes,) + plane), whole((radius,) + plane), whole((radius,) + plane)],
            scratch_shapes=work(planes + reach),
            compiler_params=params,
            cost_estimate=cost(1),
            name=f"forward{m}",
        )(before, estimate, after, measured, *mats)
        extended.append((lax.ppermute(tail, "slab", up), ratio, lax.ppermute(head, "slab", down)))

    def backward(views, first, count, running, after, name):
        operands, specs = [], []
        for m in views:
            operands += list(extended[m]) + [scale] + list(mats)
            specs += [whole(a.shape) for a in extended[m]]
            if first % count:
                raise ValueError("chunk start")
            specs.append(pl.BlockSpec((None, count * chunk) + plane, lambda *_, m=m: (m, first // count, 0, 0)))
            specs += [slot_of(a, 2 * m + 1) for a in mats]
        if running is not None:
            source, place = running
            operands.append(source)
            specs.append(pl.BlockSpec((chunk,) + plane, lambda *_: (place, 0, 0)))
        if after is not None:
            operands.append(after)
            specs.append(pl.BlockSpec(memory_space=pl.ANY))
        return pl.pallas_call(
            functools.partial(backward_kernel, chunk, reach, first, count, len(views), running is not None, after is not None),
            grid=(1,),
            out_shape=struct((count * chunk,) + plane, f32),
            in_specs=specs,
            out_specs=whole((count * chunk,) + plane),
            scratch_shapes=work(count * chunk + reach),
            compiler_params=params,
            cost_estimate=cost(len(views) * count / chunks),
            name=name,
        )(*operands)

    early = min(2, chunks) if members > 1 else 0
    every = list(range(members))
    previous = None
    if early:
        previous = partial = backward(every[:-1], 0, early, None, None, "back_early")
    pieces = []
    for c in range(chunks):
        if c < early:
            previous = backward(every[-1:], c, 1, (partial, c), previous if c else None, f"back{c}")
        else:
            previous = backward(every, c, 1, None, previous, f"back{c}")
        pieces.append(previous)

    return jnp.concatenate([summed_over(piece, "view") for piece in pieces], axis=0)


def summed_over(piece, axis):
    count = lax.axis_size(axis)
    if count == 1:
        return piece
    if count % 2:
        return lax.psum(piece, axis)
    half = count // 2
    place = lax.axis_index(axis)
    for s in range(half - 1):
        piece = piece + lax.ppermute(piece, axis, [(s, s + 1), (count - 1 - s, count - 2 - s)])
    piece = piece + lax.ppermute(piece, axis, [(half - 1, half), (half, half - 1)])
    for s in range(half - 1):
        low, high = half - 2 - s, half + 1 + s
        moved = lax.ppermute(piece, axis, [(low + 1, low), (high - 1, high)])
        piece = jnp.where((place == low) | (place == high), moved, piece)
    return piece


def solution(mesh):
    placed = (
        P(("groups", "slab"), None, None),
        P("view", ("groups", "slab"), None, None),
        P("view", None, None),
        P("view", None, None),
        P("view", None, None),
        P(),
        P(),
    )
    return jax.shard_map(
        per_device,
        mesh=mesh,
        in_specs=placed,
        out_specs=P(("groups", "slab"), None, None),
        check_vma=False,
    )
```

```python
import functools

import jax
import jax.numpy as jnp
from jax import lax
from jax.experimental import pallas as pl
from jax.experimental.pallas import tpu as pltpu
from jax.sharding import PartitionSpec as P


f32 = jnp.float32
bf16 = jnp.bfloat16
SUB = 8
VMEM_LIMIT = 13 * 2**20


def split(values):
    high = values.astype(bf16)
    return high, (values - high.astype(f32)).astype(bf16)


def dot(a, b):
    return jnp.dot(a, b, preferred_element_type=f32)


def skew(row, rows, shift):
    width = row.shape[1]
    full = jnp.broadcast_to(row, (rows, width))
    return pltpu.roll(full, shift % width, 1, stride=1, stride_axis=0)


def tap_row(ref, place, width, start, step, flip):
    taps = ref.shape[-1]
    lane = lax.broadcasted_iota(jnp.int32, (1, width), 1)
    row = jnp.zeros((1, width), f32)
    for k in range(taps):
        value = ref[place + (taps - 1 - k if flip else k,)]
        row = jnp.where(lane == start + k * step, value, row)
    return row


def prep_kernel(chunk, *refs):
    far, (est, xh, xl, ym, zm, scale), near, done = refs[:5], refs[5:11], refs[11:16], refs[16]
    copies = [pltpu.make_async_copy(a, b, done.at[i]) for i, (a, b) in enumerate(zip(far, near))]
    for copy in copies:
        copy.start()
    for copy in copies:
        copy.wait()
    psf_z, psf_y, psf_x, table, index = near
    members, rank, taps = psf_x.shape
    planes, height, width = est.shape
    radius = (taps - 1) // 2
    packed = rank * height
    first = lax.axis_index("slab") * planes
    total = lax.axis_size("slab") * planes
    view = lax.axis_index("view")

    def weight_of(v):
        code = index[v]
        weight = jnp.float32(0)
        for level in range(table.shape[0]):
            weight = weight + jnp.where(code == level, table[level], jnp.float32(0))
        return weight

    grand = jnp.float32(0)
    for v in range(index.shape[0]):
        grand = grand + weight_of(v)
    q = lax.broadcasted_iota(jnp.int32, (width, width), 0)
    p = lax.broadcasted_iota(jnp.int32, (width, width), 1)
    band = jnp.abs(p - q) <= radius
    yp = lax.broadcasted_iota(jnp.int32, (height, packed), 0)
    lane = lax.broadcasted_iota(jnp.int32, (height, packed), 1)
    yband = jnp.abs(lax.rem(lane, height) - yp) <= radius
    depth = first + lax.broadcasted_iota(jnp.int32, (planes, width), 0)
    for m in range(members):
        for way in range(2):
            slot = 2 * m + way
            flip = way == 0
            col_x = []
            for r in range(rank):
                mat = jnp.where(band, skew(tap_row(psf_x, (m, r), width, 0, 1, flip), width, -radius), 0.0)
                high, low = split(mat)
                xh[slot, r] = high
                xl[slot, r] = low
                if way:
                    col_x.append(jnp.sum(mat, axis=0, keepdims=True))
            row = jnp.zeros((1, packed), f32)
            for r in range(rank):
                row = row + tap_row(psf_y, (m, r), packed, r * height, 1, not flip)
            ymat = jnp.where(yband, skew(row, height, -radius), 0.0)
            high, low = split(ymat)
            ym[slot] = jnp.concatenate([high, low], axis=0)
            zmat = jnp.concatenate(
                [skew(tap_row(psf_z, (m, r), zm.shape[2], 0, SUB, not flip), chunk * SUB, 0) for r in range(rank)],
                axis=0,
            )
            high, low = split(zmat)
            zm[slot] = jnp.concatenate([high, low], axis=0)
        shares = []
        for r in range(rank):
            own = (lane >= r * height) & (lane < (r + 1) * height)
            col_y = jnp.sum(jnp.where(own, ymat, 0.0), axis=1, keepdims=True)
            col_z = jnp.zeros((planes, width), f32)
            for k in range(taps):
                source = depth + (radius - k)
                inside = (source >= 0) & (source < total)
                col_z = col_z + jnp.where(inside, psf_z[m, r, k], 0.0)
            shares.append((col_z, col_y * col_x[r]))
        weight = weight_of(view * members + m)
        for z in range(planes):
            normal = jnp.zeros((height, width), f32)
            for col_z, outer in shares:
                normal = normal + col_z[z : z + 1] * outer
            scale[m, z] = est[z] * (weight / (grand * normal))


def load_split(own, got, first, last, high, low):
    radius, planes = got[0].shape[0], own.shape[0]
    slab, slabs = lax.axis_index("slab"), lax.axis_size("slab")
    even = lax.rem(slab, 2) == 0

    def before(a, b, rows):
        piece = jnp.where(even, got[1][a:b, rows, :], got[0][a:b, rows, :])
        return jnp.where(slab > 0, piece, 0.0)

    def after(a, b, rows):
        piece = jnp.where(even, got[0][a:b, rows, :], got[1][a:b, rows, :])
        return jnp.where(slab < slabs - 1, piece, 0.0)

    sources = [(0, radius, before), (radius, planes, lambda a, b, rows: own[a:b, rows, :]), (radius + planes, radius, after)]
    for block in range(high.shape[0]):
        parts = []
        for start, count, read in sources:
            a, b = max(first - start, 0), min(last - start, count)
            if a < b:
                parts.append(read(a, b, slice(block * SUB, (block + 1) * SUB)))
        rows = jnp.concatenate(parts, axis=0)
        rows = rows.reshape((last - first) * SUB, rows.shape[2])
        h, l = split(rows)
        high[block, 0 : rows.shape[0]] = h
        low[block, 0 : rows.shape[0]] = l


def apply_chunk(c, chunk, reach, high, low, mats, scratch):
    xh, xl, ym, zm = mats
    dh, dl, f = scratch
    rank, width = xh.shape[0], xh.shape[1]
    blocks = high.shape[0]
    height = blocks * SUB
    depth = (chunk + reach) * SUB
    rows = chunk * SUB
    stacked = rank * rows
    zmat = zm[:, 0:depth]
    window = pl.ds(c * rows if isinstance(c, int) else pl.multiple_of(c * rows, rows), depth)
    for block in range(blocks):
        hw = high[block, window, :]
        lw = low[block, window, :]
        both = dot(zmat, hw)
        d = both[:stacked] + both[stacked:] + dot(zmat[:stacked], lw)
        for r in range(rank):
            h, l = split(d[r * rows : (r + 1) * rows])
            dh[r, block * rows : (block + 1) * rows] = h
            dl[r, block * rows : (block + 1) * rows] = l
    for r in range(rank):
        f[r] = dot(dh[r], xh[r]) + dot(dl[r], xh[r]) + dot(dh[r], xl[r])
    results = []
    for z in range(chunk):
        plane = [f[r].reshape(blocks, chunk, SUB, width)[:, z].reshape(height, width) for r in range(rank)]
        h, l = split(jnp.concatenate(plane, axis=0))
        both = dot(ym[...], h)
        results.append(both[:height] + both[height:] + dot(ym[0:height], l))
    return results


def forward_kernel(chunk, reach, est, got_a, got_b, measured, *rest):
    mats, (ratio, send_a, send_b, high, low, *scratch) = rest[:4], rest[4:]
    c = pl.program_id(0)
    planes, radius = ratio.shape[0], send_a.shape[0]

    @pl.when(c == 0)
    def _():
        load_split(est, (got_a, got_b), 0, planes + reach, high, low)

    blurred = apply_chunk(c, chunk, reach, high, low, mats, scratch)
    for z in range(chunk):
        ratio[c * chunk + z] = measured[z] / blurred[z]

    @pl.when(c == pl.num_programs(0) - 1)
    def _():
        even = lax.rem(lax.axis_index("slab"), 2) == 0
        head, tail = ratio[0:radius], ratio[planes - radius : planes]
        send_a[...] = jnp.where(even, tail, head)
        send_b[...] = jnp.where(even, head, tail)


def backward_kernel(chunk, reach, first, count, views, has_sum, has_after, *refs):
    refs = list(refs)
    take = lambda n: [refs.pop(0) for _ in range(n)]
    per_view = [(take(3), take(1)[0], take(4)) for _ in range(views)]
    running = take(1)[0] if has_sum else None
    if has_after:
        take(1)
    outs = take(len(refs) - 5)
    high, low, *scratch = refs
    step = outs[0].shape[0]
    for i, (pieces, scale, mats) in enumerate(per_view):
        load_split(pieces[0], pieces[1:], first * chunk, (first + count) * chunk + reach, high, low)
        for c in range(count):
            back = apply_chunk(c, chunk, reach, high, low, mats, scratch)
            for z in range(chunk):
                place = c * chunk + z
                out = outs[place // step]
                term = back[z] * scale[place]
                if i:
                    term = term + out[place % step]
                elif has_sum:
                    term = term + running[place]
                out[place % step] = term


def finish_kernel(got, own, *rest):
    place, count = lax.axis_index("view"), lax.axis_size("view")
    end = (place == 0) | (place == count - 1)
    rest[-1][...] = jnp.where(end, got[...], own[...])


def whole(shape):
    return pl.BlockSpec(shape, lambda *_: (0,) * len(shape))


def slot_of(array, slot):
    return pl.BlockSpec((None,) + array.shape[1:], lambda *_: (slot,) + (0,) * (array.ndim - 1))


def per_device(estimate, measured, psf_z, psf_y, psf_x, weight_table, weight_index):
    members, planes, height, width = measured.shape
    rank, taps = psf_x.shape[1:]
    reach = taps - 1
    radius = reach // 2
    chunk = next(c for c in (4, 2, 1) if planes % c == 0)
    chunks = planes // chunk
    struct = jax.ShapeDtypeStruct
    plane = (height, width)
    params = pltpu.CompilerParams(vmem_limit_bytes=VMEM_LIMIT)
    small = [pltpu.with_memory_space_constraint(a, pltpu.HBM) for a in (psf_z, psf_y, psf_x, weight_table, weight_index)]

    def cost(fraction):
        flops = 2 * 6912 * 65536 * chunks * fraction
        return pl.CostEstimate(flops=int(flops), bytes_accessed=int(4e6), transcendentals=0)

    slabs, line = lax.axis_size("slab"), lax.axis_size("view")
    even = lax.rem(lax.axis_index("slab"), 2) == 0
    across = [swaps(slabs, line, 0, 0), swaps(slabs, line, 0, 1)]
    along = [swaps(slabs, line, 1, 0), swaps(slabs, line, 1, 1)]

    def exchange(send, perm, name):
        with jax.named_scope(name):
            return lax.ppermute(send, ("slab", "view"), perm)

    head, tail = estimate[:radius], estimate[planes - radius :]
    got = [
        exchange(jnp.where(even, tail, head), across[0], "est_a"),
        exchange(jnp.where(even, head, tail), across[1], "est_b"),
    ]
    depth_lanes = -(-(chunk + reach) * SUB // 128) * 128
    slots = 2 * members
    mats_and_scale = pl.pallas_call(
        functools.partial(prep_kernel, chunk),
        out_shape=[
            struct((slots, rank, width, width), bf16),
            struct((slots, rank, width, width), bf16),
            struct((slots, 2 * height, rank * height), bf16),
            struct((slots, 2 * rank * chunk * SUB, depth_lanes), bf16),
            struct((members, planes) + plane, f32),
        ],
        in_specs=[pl.BlockSpec(memory_space=pltpu.HBM)] * 5 + [pl.BlockSpec(memory_space=pltpu.VMEM)],
        scratch_shapes=[pltpu.SMEM(a.shape, a.dtype) for a in small] + [pltpu.SemaphoreType.DMA((len(small),))],
        compiler_params=params,
        cost_estimate=cost(0.7),
        name="prep",
    )(*small, estimate)
    mats, scale = mats_and_scale[:4], mats_and_scale[4]

    def work(window):
        return [
            pltpu.VMEM((height // SUB, window * SUB, width), bf16),
            pltpu.VMEM((height // SUB, window * SUB, width), bf16),
            pltpu.VMEM((rank, height * chunk, width), bf16),
            pltpu.VMEM((rank, height * chunk, width), bf16),
            pltpu.VMEM((rank, height * chunk, width), f32),
        ]

    extended = []
    for m in range(members):
        with jax.named_scope(f"fwd{m}"):
            ratio, send_a, send_b = pl.pallas_call(
                functools.partial(forward_kernel, chunk, reach),
                grid=(chunks,),
                out_shape=[struct((planes,) + plane, f32), struct((radius,) + plane, f32), struct((radius,) + plane, f32)],
                in_specs=[
                    whole(estimate.shape),
                    whole(got[0].shape),
                    whole(got[1].shape),
                    pl.BlockSpec((None, chunk) + plane, lambda c, m=m: (m, c, 0, 0)),
                ]
                + [slot_of(a, 2 * m) for a in mats],
                out_specs=[whole((planes,) + plane), whole((radius,) + plane), whole((radius,) + plane)],
                scratch_shapes=work(planes + reach),
                compiler_params=params,
                cost_estimate=cost(1),
                name=f"forward{m}",
            )(estimate, *got, measured, *mats)
        extended.append(
            (ratio, exchange(send_a, across[0], f"ratio{m}_a"), exchange(send_b, across[1], f"ratio{m}_b"))
        )

    def backward(views, first, count, running, after, piece, name):
        operands, specs = [], []
        for m in views:
            operands += list(extended[m]) + [scale] + list(mats)
            specs += [whole(a.shape) for a in extended[m]]
            if first % count:
                raise ValueError("chunk start")
            specs.append(pl.BlockSpec((None, count * chunk) + plane, lambda *_, m=m: (m, first // count, 0, 0)))
            specs += [slot_of(a, 2 * m + 1) for a in mats]
        if running is not None:
            source, place = running
            operands.append(source)
            specs.append(pl.BlockSpec((count * chunk,) + plane, lambda *_: (place // count, 0, 0)))
        if after is not None:
            operands.append(after)
            specs.append(pl.BlockSpec(memory_space=pltpu.HBM))
        shapes = [(piece,) + plane] * (count * chunk // piece)
        with jax.named_scope(name):
            return pl.pallas_call(
                functools.partial(backward_kernel, chunk, reach, first, count, len(views), running is not None, after is not None),
                grid=(1,),
                out_shape=[struct(shape, f32) for shape in shapes],
                in_specs=specs,
                out_specs=[whole(shape) for shape in shapes],
                scratch_shapes=work(count * chunk + reach),
                compiler_params=params,
                cost_estimate=cost(len(views) * count / chunks),
                name=name,
            )(*operands)

    every = list(range(members))
    previous = partial = None
    if members > 1:
        (partial,) = backward(every[:-1], 0, chunks, None, None, planes, "early")
        previous = partial
    small_piece = max(chunk // 2, 1)
    pieces = []
    for c in range(chunks):
        pieces += backward(
            every[-1:], c, 1, None if partial is None else (partial, c), previous if c else None, small_piece, f"back{c}"
        )
        previous = pieces[-1]
    return line_sum(pieces, along, exchange, (planes,) + plane)


LAG = 3


def line_sum(pieces, along, exchange, shape):
    count = lax.axis_size("view")
    sizes = [piece.shape[0] for piece in pieces]
    if count == 1:
        return jnp.concatenate(pieces, axis=0)
    if count % 2:
        return lax.psum(jnp.concatenate(pieces, axis=0), "view")
    half = count // 2
    last = 2 * half - 2
    place = lax.axis_index("view")
    depth = jnp.minimum(place, count - 1 - place)
    pieces = list(pieces)
    total = len(pieces)
    out = None
    for j in range(total + (last // 2) * LAG):
        for odd in range(2):
            live = [(j - (i // 2) * LAG, i) for i in range(odd, last + 1, 2)]
            live = [(k, i) for k, i in live if 0 <= k < total]
            if not live:
                continue
            send = pieces[live[0][0]]
            for k, i in live[1:]:
                sender = i if i < half else 2 * half - 1 - i
                send = jnp.where(depth == sender, pieces[k], send)
            got = exchange(send, along[odd], f"{'mid' if odd else 'out'}{j}x")
            for k, i in live:
                if i < half:
                    target = min(i + 1, half - 1)
                    pieces[k] = jnp.where(depth == target, pieces[k] + got, pieces[k])
                elif i < last:
                    pieces[k] = jnp.where(depth == last - i, got, pieces[k])
                if i == last:
                    out = finish(got if half > 1 else pieces[k], pieces[k], out, k, shape)
    return out


def finish(got, own, out, k, shape):
    block = pl.BlockSpec(own.shape, lambda *_: (k, 0, 0))
    with jax.named_scope(f"finish{k}x"):
        return pl.pallas_call(
            finish_kernel,
            grid=(1,),
            out_shape=jax.ShapeDtypeStruct(shape, f32),
            in_specs=[whole(got.shape), whole(own.shape)] + ([pl.BlockSpec(memory_space=pltpu.HBM)] if out is not None else []),
            out_specs=block,
            input_output_aliases={2: 0} if out is not None else {},
            compiler_params=pltpu.CompilerParams(vmem_limit_bytes=2**22),
            cost_estimate=pl.CostEstimate(flops=1000, bytes_accessed=12 * own.size, transcendentals=0),
            name=f"finish{k}",
        )(got, own, *([] if out is None else [out]))


def swaps(slabs, line, axis, odd):
    pairs = []
    for s in range(slabs):
        for v in range(line):
            here, sizes = [s, v], (slabs, line)
            there = list(here)
            step = 1 if (here[axis] - odd) % 2 == 0 else -1
            if 0 <= here[axis] + step < sizes[axis]:
                there[axis] += step
            else:
                other = 1 - axis
                step = 1 if here[other] % 2 == 0 else -1
                if 0 <= here[other] + step < sizes[other]:
                    there[other] += step
            pairs.append((s * line + v, there[0] * line + there[1]))
    return pairs


def solution(mesh):
    placed = (
        P(("groups", "slab"), None, None),
        P("view", ("groups", "slab"), None, None),
        P("view", None, None),
        P("view", None, None),
        P("view", None, None),
        P(),
        P(),
    )
    return jax.shard_map(
        per_device,
        mesh=mesh,
        in_specs=placed,
        out_specs=P(("groups", "slab"), None, None),
        check_vma=False,
    )
```

```python
import functools

import jax
import jax.numpy as jnp
from jax import lax
from jax.experimental import pallas as pl
from jax.experimental.pallas import tpu as pltpu
from jax.sharding import PartitionSpec as P


f32 = jnp.float32
bf16 = jnp.bfloat16
SUB = 8
VMEM_LIMIT = 24 * 2**20


def split(values):
    high = values.astype(bf16)
    return high, (values - high.astype(f32)).astype(bf16)


def dot(a, b):
    return jnp.dot(a, b, preferred_element_type=f32)


def skew(row, rows, shift):
    width = row.shape[1]
    full = jnp.broadcast_to(row, (rows, width))
    return pltpu.roll(full, shift % width, 1, stride=1, stride_axis=0)


def tap_row(ref, place, width, start, step, flip):
    taps = ref.shape[-1]
    lane = lax.broadcasted_iota(jnp.int32, (1, width), 1)
    row = jnp.zeros((1, width), f32)
    for k in range(taps):
        value = ref[place + (taps - 1 - k if flip else k,)]
        row = jnp.where(lane == start + k * step, value, row)
    return row


def prep_kernel(chunk, *refs):
    far, (est, xh, xl, ym, zm, scale), near, done = refs[:5], refs[5:11], refs[11:16], refs[16]
    copies = [pltpu.make_async_copy(a, b, done.at[i]) for i, (a, b) in enumerate(zip(far, near))]
    for copy in copies:
        copy.start()
    for copy in copies:
        copy.wait()
    psf_z, psf_y, psf_x, table, index = near
    members, rank, taps = psf_x.shape
    planes, height, width = est.shape
    radius = (taps - 1) // 2
    packed = rank * height
    first = lax.axis_index("slab") * planes
    total = lax.axis_size("slab") * planes
    view = lax.axis_index("view")

    def weight_of(v):
        code = index[v]
        weight = jnp.float32(0)
        for level in range(table.shape[0]):
            weight = weight + jnp.where(code == level, table[level], jnp.float32(0))
        return weight

    grand = jnp.float32(0)
    for v in range(index.shape[0]):
        grand = grand + weight_of(v)
    q = lax.broadcasted_iota(jnp.int32, (width, width), 0)
    p = lax.broadcasted_iota(jnp.int32, (width, width), 1)
    band = jnp.abs(p - q) <= radius
    yp = lax.broadcasted_iota(jnp.int32, (height, packed), 0)
    lane = lax.broadcasted_iota(jnp.int32, (height, packed), 1)
    yband = jnp.abs(lax.rem(lane, height) - yp) <= radius
    depth = first + lax.broadcasted_iota(jnp.int32, (planes, width), 0)
    for m in range(members):
        for way in range(2):
            slot = 2 * m + way
            flip = way == 0
            col_x = []
            for r in range(rank):
                mat = jnp.where(band, skew(tap_row(psf_x, (m, r), width, 0, 1, flip), width, -radius), 0.0)
                high, low = split(mat)
                xh[slot, r] = high
                xl[slot, r] = low
                if way:
                    col_x.append(jnp.sum(mat, axis=0, keepdims=True))
            row = jnp.zeros((1, packed), f32)
            for r in range(rank):
                row = row + tap_row(psf_y, (m, r), packed, r * height, 1, not flip)
            ymat = jnp.where(yband, skew(row, height, -radius), 0.0)
            high, low = split(ymat)
            ym[slot] = jnp.concatenate([high, low], axis=0)
            zmat = jnp.concatenate(
                [skew(tap_row(psf_z, (m, r), zm.shape[2], 0, SUB, not flip), chunk * SUB, 0) for r in range(rank)],
                axis=0,
            )
            high, low = split(zmat)
            zm[slot] = jnp.concatenate([high, low], axis=0)
        shares = []
        for r in range(rank):
            own = (lane >= r * height) & (lane < (r + 1) * height)
            col_y = jnp.sum(jnp.where(own, ymat, 0.0), axis=1, keepdims=True)
            col_z = jnp.zeros((planes, width), f32)
            for k in range(taps):
                source = depth + (radius - k)
                inside = (source >= 0) & (source < total)
                col_z = col_z + jnp.where(inside, psf_z[m, r, k], 0.0)
            shares.append((col_z, col_y * col_x[r]))
        weight = weight_of(view * members + m)
        for z in range(planes):
            normal = jnp.zeros((height, width), f32)
            for col_z, outer in shares:
                normal = normal + col_z[z : z + 1] * outer
            scale[m, z] = est[z] * (weight / (grand * normal))


def load_split(pieces, first, last, high, low):
    starts = [0]
    for piece in pieces:
        starts.append(starts[-1] + piece.shape[0])
    for block in range(high.shape[0]):
        parts = []
        for piece, start in zip(pieces, starts):
            a, b = max(first - start, 0), min(last - start, piece.shape[0])
            if a < b:
                parts.append(piece[a:b, block * SUB : (block + 1) * SUB, :])
        rows = jnp.concatenate(parts, axis=0)
        rows = rows.reshape((last - first) * SUB, rows.shape[2])
        h, l = split(rows)
        high[block, 0 : rows.shape[0]] = h
        low[block, 0 : rows.shape[0]] = l


def apply_chunk(c, chunk, reach, high, low, mats, scratch):
    xh, xl, ym, zm = mats
    dh, dl, f = scratch
    rank, width = xh.shape[0], xh.shape[1]
    blocks = high.shape[0]
    height = blocks * SUB
    depth = (chunk + reach) * SUB
    rows = chunk * SUB
    stacked = rank * rows
    zmat = zm[:, 0:depth]
    window = pl.ds(c * rows if isinstance(c, int) else pl.multiple_of(c * rows, rows), depth)
    for block in range(blocks):
        hw = high[block, window, :]
        lw = low[block, window, :]
        both = dot(zmat, hw)
        d = both[:stacked] + both[stacked:] + dot(zmat[:stacked], lw)
        for r in range(rank):
            h, l = split(d[r * rows : (r + 1) * rows])
            dh[r, block * rows : (block + 1) * rows] = h
            dl[r, block * rows : (block + 1) * rows] = l
    for r in range(rank):
        f[r] = dot(dh[r], xh[r]) + dot(dl[r], xh[r]) + dot(dh[r], xl[r])
    results = []
    for z in range(chunk):
        plane = [f[r].reshape(blocks, chunk, SUB, width)[:, z].reshape(height, width) for r in range(rank)]
        h, l = split(jnp.concatenate(plane, axis=0))
        both = dot(ym[...], h)
        results.append(both[:height] + both[height:] + dot(ym[0:height], l))
    return results


def forward_kernel(chunk, reach, before, est, after, measured, *rest):
    mats, (ratio, head, tail, high, low, *scratch) = rest[:4], rest[4:]
    c = pl.program_id(0)
    planes = ratio.shape[0]

    @pl.when(c == 0)
    def _():
        load_split((before, est, after), 0, planes + reach, high, low)

    blurred = apply_chunk(c, chunk, reach, high, low, mats, scratch)
    for z in range(chunk):
        ratio[c * chunk + z] = measured[z] / blurred[z]

    @pl.when(c == pl.num_programs(0) - 1)
    def _():
        head[...] = ratio[0 : head.shape[0]]
        tail[...] = ratio[planes - tail.shape[0] : planes]


def backward_kernel(chunk, reach, first, count, views, has_sum, has_after, *refs):
    refs = list(refs)
    take = lambda n: [refs.pop(0) for _ in range(n)]
    per_view = [(take(3), take(1)[0], take(4)) for _ in range(views)]
    running = take(1)[0] if has_sum else None
    if has_after:
        take(1)
    outs = take(len(refs) - 5)
    high, low, *scratch = refs
    step = outs[0].shape[0]
    for i, (pieces, scale, mats) in enumerate(per_view):
        load_split(pieces, first * chunk, (first + count) * chunk + reach, high, low)
        for c in range(count):
            back = apply_chunk(c, chunk, reach, high, low, mats, scratch)
            for z in range(chunk):
                place = c * chunk + z
                out = outs[place // step]
                term = back[z] * scale[place]
                if i:
                    term = term + out[place % step]
                elif has_sum:
                    term = term + running[place]
                out[place % step] = term


def whole(shape):
    return pl.BlockSpec(shape, lambda *_: (0,) * len(shape))


def slot_of(array, slot):
    return pl.BlockSpec((None,) + array.shape[1:], lambda *_: (slot,) + (0,) * (array.ndim - 1))


def per_device(estimate, measured, psf_z, psf_y, psf_x, weight_table, weight_index):
    members, planes, height, width = measured.shape
    rank, taps = psf_x.shape[1:]
    reach = taps - 1
    radius = reach // 2
    chunk = next(c for c in (4, 2, 1) if planes % c == 0)
    chunks = planes // chunk
    struct = jax.ShapeDtypeStruct
    plane = (height, width)
    params = pltpu.CompilerParams(vmem_limit_bytes=VMEM_LIMIT)
    small = [pltpu.with_memory_space_constraint(a, pltpu.HBM) for a in (psf_z, psf_y, psf_x, weight_table, weight_index)]

    def cost(fraction):
        flops = 2 * 6912 * 65536 * chunks * fraction
        return pl.CostEstimate(flops=int(flops), bytes_accessed=int(4e6), transcendentals=0)

    slabs, line = lax.axis_size("slab"), lax.axis_size("view")
    slab = lax.axis_index("slab")
    even = lax.rem(slab, 2) == 0
    across = [swaps(slabs, line, 0, 0), swaps(slabs, line, 0, 1)]
    along = [swaps(slabs, line, 1, 0), swaps(slabs, line, 1, 1)]

    def exchange(send, perm, name):
        with jax.named_scope(name):
            return lax.ppermute(send, ("slab", "view"), perm)

    def neighbours(head, tail, name):
        got_a = exchange(jnp.where(even, tail, head), across[0], name + "_a")
        got_b = exchange(jnp.where(even, head, tail), across[1], name + "_b")
        before = jnp.where(slab > 0, jnp.where(even, got_b, got_a), 0.0)
        after = jnp.where(slab < slabs - 1, jnp.where(even, got_a, got_b), 0.0)
        return before, after

    before, after = neighbours(estimate[:radius], estimate[planes - radius :], "est")
    depth_lanes = -(-(chunk + reach) * SUB // 128) * 128
    slots = 2 * members
    mats_and_scale = pl.pallas_call(
        functools.partial(prep_kernel, chunk),
        out_shape=[
            struct((slots, rank, width, width), bf16),
            struct((slots, rank, width, width), bf16),
            struct((slots, 2 * height, rank * height), bf16),
            struct((slots, 2 * rank * chunk * SUB, depth_lanes), bf16),
            struct((members, planes) + plane, f32),
        ],
        in_specs=[pl.BlockSpec(memory_space=pltpu.HBM)] * 5 + [pl.BlockSpec(memory_space=pltpu.VMEM)],
        scratch_shapes=[pltpu.SMEM(a.shape, a.dtype) for a in small] + [pltpu.SemaphoreType.DMA((len(small),))],
        compiler_params=params,
        cost_estimate=cost(0.7),
        name="prep",
    )(*small, estimate)
    mats, scale = mats_and_scale[:4], mats_and_scale[4]

    def work(window):
        return [
            pltpu.VMEM((height // SUB, window * SUB, width), bf16),
            pltpu.VMEM((height // SUB, window * SUB, width), bf16),
            pltpu.VMEM((rank, height * chunk, width), bf16),
            pltpu.VMEM((rank, height * chunk, width), bf16),
            pltpu.VMEM((rank, height * chunk, width), f32),
        ]

    extended = []
    for m in range(members):
        with jax.named_scope(f"fwd{m}"):
            ratio, head, tail = pl.pallas_call(
                functools.partial(forward_kernel, chunk, reach),
                grid=(chunks,),
                out_shape=[struct((planes,) + plane, f32), struct((radius,) + plane, f32), struct((radius,) + plane, f32)],
                in_specs=[
                    whole(before.shape),
                    whole(estimate.shape),
                    whole(after.shape),
                    pl.BlockSpec((None, chunk) + plane, lambda c, m=m: (m, c, 0, 0)),
                ]
                + [slot_of(a, 2 * m) for a in mats],
                out_specs=[whole((planes,) + plane), whole((radius,) + plane), whole((radius,) + plane)],
                scratch_shapes=work(planes + reach),
                compiler_params=params,
                cost_estimate=cost(1),
                name=f"forward{m}",
            )(before, estimate, after, measured, *mats)
        left, right = neighbours(head, tail, f"ratio{m}")
        extended.append((left, ratio, right))

    def backward(views, first, count, running, after, piece, name):
        operands, specs = [], []
        for m in views:
            operands += list(extended[m]) + [scale] + list(mats)
            specs += [whole(a.shape) for a in extended[m]]
            if first % count:
                raise ValueError("chunk start")
            specs.append(pl.BlockSpec((None, count * chunk) + plane, lambda *_, m=m: (m, first // count, 0, 0)))
            specs += [slot_of(a, 2 * m + 1) for a in mats]
        if running is not None:
            source, place = running
            operands.append(source)
            specs.append(pl.BlockSpec((count * chunk,) + plane, lambda *_: (place // count, 0, 0)))
        if after is not None:
            operands.append(after)
            specs.append(pl.BlockSpec(memory_space=pltpu.HBM))
        shapes = [(piece,) + plane] * (count * chunk // piece)
        with jax.named_scope(name):
            return pl.pallas_call(
                functools.partial(backward_kernel, chunk, reach, first, count, len(views), running is not None, after is not None),
                grid=(1,),
                out_shape=[struct(shape, f32) for shape in shapes],
                in_specs=specs,
                out_specs=[whole(shape) for shape in shapes],
                scratch_shapes=work(count * chunk + reach),
                compiler_params=params,
                cost_estimate=cost(len(views) * count / chunks),
                name=name,
            )(*operands)

    every = list(range(members))
    previous = partial = None
    if members > 1:
        (partial,) = backward(every[:-1], 0, chunks, None, None, planes, "early")
        previous = partial
    small_piece = max(chunk // 2, 1)
    pieces = []
    for c in range(chunks):
        pieces += backward(
            every[-1:], c, 1, None if partial is None else (partial, c), previous if c else None, small_piece, f"back{c}"
        )
        previous = pieces[-1]
    return line_sum(pieces, along, exchange, (planes,) + plane)


LAG = 3


def line_sum(pieces, along, exchange, shape):
    count = lax.axis_size("view")
    sizes = [piece.shape[0] for piece in pieces]
    if count == 1:
        return jnp.concatenate(pieces, axis=0)
    if count % 2:
        return lax.psum(jnp.concatenate(pieces, axis=0), "view")
    half = count // 2
    last = 2 * half - 2
    place = lax.axis_index("view")
    depth = jnp.minimum(place, count - 1 - place)
    pieces = list(pieces)
    total = len(pieces)
    out = jnp.zeros(shape, f32)
    for j in range(total + (last // 2) * LAG):
        for odd in range(2):
            live = [(j - (i // 2) * LAG, i) for i in range(odd, last + 1, 2)]
            live = [(k, i) for k, i in live if 0 <= k < total]
            if not live:
                continue
            send = pieces[live[0][0]]
            for k, i in live[1:]:
                sender = i if i < half else 2 * half - 1 - i
                send = jnp.where(depth == sender, pieces[k], send)
            got = exchange(send, along[odd], f"{'mid' if odd else 'out'}{j}x")
            for k, i in live:
                if i < half:
                    target = min(i + 1, half - 1)
                    pieces[k] = jnp.where(depth == target, pieces[k] + got, pieces[k])
                elif i < last:
                    pieces[k] = jnp.where(depth == last - i, got, pieces[k])
                elif half > 1:
                    pieces[k] = jnp.where(depth == 0, got, pieces[k])
                if i == last:
                    out = lax.dynamic_update_slice(out, pieces[k], (sum(sizes[:k]), 0, 0))
    return out


def swaps(slabs, line, axis, odd):
    pairs = []
    for s in range(slabs):
        for v in range(line):
            here, sizes = [s, v], (slabs, line)
            there = list(here)
            step = 1 if (here[axis] - odd) % 2 == 0 else -1
            if 0 <= here[axis] + step < sizes[axis]:
                there[axis] += step
            else:
                other = 1 - axis
                step = 1 if here[other] % 2 == 0 else -1
                if 0 <= here[other] + step < sizes[other]:
                    there[other] += step
            pairs.append((s * line + v, there[0] * line + there[1]))
    return pairs


def solution(mesh):
    placed = (
        P(("groups", "slab"), None, None),
        P("view", ("groups", "slab"), None, None),
        P("view", None, None),
        P("view", None, None),
        P("view", None, None),
        P(),
        P(),
    )
    return jax.shard_map(
        per_device,
        mesh=mesh,
        in_specs=placed,
        out_specs=P(("groups", "slab"), None, None),
        check_vma=False,
    )
```
